32 devices in a mesh: fsdp: 4 (over z), rep: 8 (over y, x, core).
Axes of the slice: x: 2, y: 2, z: 4, core: 2. Of those that a mesh axis runs over, the one named last changes fastest.
Arguments:
- tokens: bfloat16 [8, 512, 2048], P('rep', 'fsdp'), may hold values from -6 to 6
- cotangent: bfloat16 [8, 512, 2048], P('rep', 'fsdp'), may hold values from -6 to 6
- lengths: int32 [8, 8], P('rep'), may hold values from 32 to 96, as said below
- deal_order: int32 [8, 8], P('rep'), may hold values from 0 to 7, as said below
- attn_gain: bfloat16 [2048], P('fsdp'), may hold values from 0.099609375 to 1.8984375
- mlp_gain: bfloat16 [2048], P('fsdp'), may hold values from 0.099609375 to 1.8984375
- q_scale: bfloat16 [128], P('fsdp'), may hold values from 0.099609375 to 1.8984375
- k_scale: bfloat16 [128], P('fsdp'), may hold values from 0.099609375 to 1.8984375
- w_qkv: bfloat16 [2048, 4096], P('fsdp'), may hold values from -0.125 to 0.125
- w_hgate: bfloat16 [2048, 16], P('fsdp'), may hold values from -0.125 to 0.125
- w_out: bfloat16 [2048, 2048], P('fsdp'), may hold values from -1.5 to 1.5
- w_gate: bfloat16 [2048, 6144], P('fsdp'), may hold values from -0.125 to 0.125
- w_up: bfloat16 [2048, 6144], P('fsdp'), may hold values from -0.125 to 0.125
- w_down: bfloat16 [2048, 6144], P('fsdp'), may hold values from -0.078125 to 0.078125
Outputs:
- output: bfloat16 [8, 512, 2048], P('rep', 'fsdp')
- tokens_grad: bfloat16 [8, 512, 2048], P('rep', 'fsdp')
- attn_gain_grad: float32 [2048], P('fsdp')
- mlp_gain_grad: float32 [2048], P('fsdp')
- q_scale_grad: float32 [128], P('fsdp')
- k_scale_grad: float32 [128], P('fsdp')
- w_qkv_grad: float32 [2048, 4096], P('fsdp')
- w_hgate_grad: float32 [2048, 16], P('fsdp')
- w_out_grad: float32 [2048, 2048], P('fsdp')
- w_gate_grad: float32 [2048, 6144], P('fsdp')
- w_up_grad: float32 [2048, 6144], P('fsdp')
- w_down_grad: float32 [2048, 6144], P('fsdp')
The draws below stay inside these ranges and needn't reach their ends.
Inputs may be any that keep to these rules, and one draw needn't show every extreme that they name: `lengths`: every length is a multiple of 32; the 2 sequences dealt to each index of fsdp hold 128 tokens together. `deal_order`: each row is a permutation of the group's sequences.
All inputs are finite; a program needn't handle non-finite values.
Results may differ from the reference program's by a relative error of at most 0.015.
Values may be sent and summed in bfloat16 or wider, within the bound.
A program may use at most 704 MiB of HBM per device.

```python
import jax
import jax.numpy as jnp
from jax import lax

D = 2048
QUERY_HEADS = 16
KEY_VALUE_HEADS = 8
HEAD_SIZE = 128
FF = 6144
TOK_DEV = 128
SEQ_DEV = 2
UNIT = 32
GROUP_TOK = 512
QKV = 4096
N_FSDP = 4
N_REP = 8


def dealt_plan(key):
    unit_count = TOK_DEV // UNIT

    def one_group(group_key):
        first_part = jax.random.randint(jax.random.fold_in(group_key, 1), (N_FSDP,), 1, unit_count)
        longest = jax.random.randint(jax.random.fold_in(group_key, 2), (), 0, N_FSDP)
        first_part = jnp.where(jnp.arange(N_FSDP) == longest, unit_count - 1, first_part)
        dealt_lengths = (jnp.stack([first_part, unit_count - first_part], axis=1).reshape(-1) * UNIT).astype(jnp.int32)
        order_row = jax.random.permutation(jax.random.fold_in(group_key, 3), N_FSDP * SEQ_DEV).astype(jnp.int32)
        lengths_row = jnp.zeros((N_FSDP * SEQ_DEV,), jnp.int32).at[order_row].set(dealt_lengths)
        return (lengths_row, order_row)

    def group_key_of(index):
        return jax.random.fold_in(jax.random.fold_in(key, 77), index)
    group_keys = jax.vmap(group_key_of)(jnp.arange(N_REP))
    return jax.vmap(one_group)(group_keys)


def draw_lengths(key, part):
    return dealt_plan(key)[0]


def draw_deal_order(key, part):
    return dealt_plan(key)[1]


def raised(values, own_key, source, target, parts, factor):
    owner, partner = [(jnp.arange(values.shape[dim]) // (values.shape[dim] // parts)).reshape([-1 if axis == dim else 1 for axis in range(values.ndim)]) for dim in (source, target)]
    chosen = jax.random.permutation(own_key, parts)[partner]
    strong = (owner == chosen) | (owner == (partner + parts // 2) % parts)
    return jnp.where(strong, factor * values, values)


def steps_of(stream_key, shape, cuts, low, top_value):
    level = 1.0
    for dim, parts in cuts:
        steps = jax.random.uniform(jax.random.fold_in(jax.random.fold_in(stream_key, 6), dim), (parts,), jnp.float32, low / len(cuts), top_value / len(cuts))
        level = level * jnp.repeat(jnp.exp(steps), shape[dim] // parts).reshape((-1,) + (1,) * (len(shape) - 1 - dim))
    return level


def normal_values(key, shape, spread, bound, shards=(), kind=jnp.bfloat16):
    values = spread * jax.random.normal(key, shape, jnp.float32)
    if shards:
        values = values * steps_of(key, shape, shards, -0.22, 0.18)
    return jnp.clip(values, -bound, bound).astype(kind)


def noise_with(stream_key, dims, deviation, reach, cuts, heavy, kind=jnp.bfloat16):
    drawn = deviation * jax.random.normal(stream_key, dims, jnp.float32)
    if cuts:
        drawn = drawn * steps_of(stream_key, dims, cuts, -0.22, 0.18)
    return jnp.clip(raised(drawn, jax.random.fold_in(stream_key, 3), *heavy), -reach, reach).astype(kind)


def setup_inputs(seed: int = 0) -> dict:
    key_list = jax.random.split(jax.random.key(seed), 15)
    return {
        "tokens": normal_values(key_list[0], (N_REP, GROUP_TOK, D), 1.0, 6.0, ((0, 8), (1, 4))),
        "cotangent": noise_with(key_list[1], (N_REP, GROUP_TOK, D), 1.0, 6.0, ((0, 8), (1, 4)), (1, 2, 4, 2.0)),
        "lengths": draw_lengths(jax.random.fold_in(key_list[14], 71), 0),
        "deal_order": draw_deal_order(jax.random.fold_in(key_list[14], 71), 0),
        "attn_gain": jnp.clip(1.0 + 0.18 * jax.random.normal(key_list[4], (D,), jnp.float32), 0.099609375, 1.8984375).astype(jnp.bfloat16),
        "mlp_gain": jnp.clip(1.0 + 0.18 * jax.random.normal(key_list[5], (D,), jnp.float32), 0.099609375, 1.8984375).astype(jnp.bfloat16),
        "q_scale": jnp.clip(1.0 + 0.18 * jax.random.normal(key_list[6], (HEAD_SIZE,), jnp.float32), 0.099609375, 1.8984375).astype(jnp.bfloat16),
        "k_scale": jnp.clip(1.0 + 0.18 * jax.random.normal(key_list[7], (HEAD_SIZE,), jnp.float32), 0.099609375, 1.8984375).astype(jnp.bfloat16),
        "w_qkv": normal_values(key_list[8], (D, QKV), D ** -0.5, 0.125, ((0, 4),)),
        "w_hgate": normal_values(key_list[9], (D, QUERY_HEADS), D ** -0.5, 0.125, ((0, 4),)),
        "w_out": normal_values(key_list[10], (D, QUERY_HEADS * HEAD_SIZE), (max(QUERY_HEADS * HEAD_SIZE // 128, 1)) ** -0.5, 1.5, ((0, 4),)),
        "w_gate": normal_values(key_list[11], (D, FF), D ** -0.5, 0.125, ((0, 4),)),
        "w_up": normal_values(key_list[12], (D, FF), D ** -0.5, 0.125, ((0, 4),)),
        "w_down": normal_values(key_list[13], (D, FF), FF ** -0.5, 0.078125, ((0, 4),)),
    }


eps_norm = 1e-06
rope_base = 1000000.0

@jax.custom_vjp
def lower_precision(v):
    return lax.optimization_barrier(v.astype(jnp.bfloat16)).astype(jnp.float32)

@jax.custom_vjp
def low_back(v):
    return v

def low_keep(v):
    return (lower_precision(v), None)

def low_pass(kept, grad):
    return (grad,)

def back_keep(v):
    return (v, None)

def back_low(kept, grad):
    return (lower_precision(grad),)
lower_precision.defvjp(low_keep, low_pass)
low_back.defvjp(back_keep, back_low)

def product(left, right):
    return jnp.dot(left, right, precision=lax.Precision.HIGHEST, preferred_element_type=jnp.float32)

def normalize(value_rows, gain):
    return value_rows * lax.rsqrt(lax.optimization_barrier(jnp.mean(value_rows * value_rows, axis=-1, keepdims=True)) + eps_norm) * gain

def rope_tables(positions):
    half_dim = HEAD_SIZE // 2
    frequency = jnp.power(rope_base, -2.0 * jnp.arange(half_dim, dtype=jnp.float32) / HEAD_SIZE)
    angles = positions.astype(jnp.float32)[:, None] * frequency[None, :]
    angles = jnp.concatenate([angles, angles], axis=1)
    return (jnp.cos(angles)[:, None, :], jnp.sin(angles)[:, None, :])

def rotate(value_rows, cosine, sine_table):
    half_dim = value_rows.shape[-1] // 2
    turned = jnp.concatenate([-value_rows[..., half_dim:], value_rows[..., :half_dim]], axis=-1)
    return value_rows * cosine + turned * sine_table

def deal_map(group_lengths, group_order):
    starts = (jnp.cumsum(group_lengths) - group_lengths).astype(jnp.int32)
    dealt_lengths = group_lengths[group_order].astype(jnp.int32)
    dealt_starts = (jnp.cumsum(dealt_lengths) - dealt_lengths).astype(jnp.int32)
    row_index = jnp.arange(N_FSDP * TOK_DEV, dtype=jnp.int32)
    segment = lax.optimization_barrier(jnp.sum((row_index[:, None] >= dealt_starts[None, 1:]).astype(jnp.int32), axis=1)).astype(jnp.int32)
    position = (row_index - dealt_starts[segment]).astype(jnp.int32)
    source = (starts[group_order[segment]] + position).astype(jnp.int32)
    return (source, segment, position)

def attend(block_projected, segment, position, q_scale, k_scale):
    count_of_rows = block_projected.shape[0]
    group_list = QUERY_HEADS // KEY_VALUE_HEADS
    query_raw = block_projected[:, :QUERY_HEADS * HEAD_SIZE].reshape(count_of_rows, QUERY_HEADS, HEAD_SIZE)
    key_unrotated = block_projected[:, QUERY_HEADS * HEAD_SIZE:(QUERY_HEADS + KEY_VALUE_HEADS) * HEAD_SIZE].reshape(count_of_rows, KEY_VALUE_HEADS, HEAD_SIZE)
    value_rows = lower_precision(block_projected[:, (QUERY_HEADS + KEY_VALUE_HEADS) * HEAD_SIZE:].reshape(count_of_rows, KEY_VALUE_HEADS, HEAD_SIZE))
    cosine, sine_table = rope_tables(position)
    queries = lower_precision(low_back(rotate(normalize(query_raw, q_scale), cosine, sine_table)))
    keys_rot = lower_precision(low_back(rotate(normalize(key_unrotated, k_scale), cosine, sine_table)))
    keys_wide = jnp.repeat(keys_rot, group_list, axis=1)
    values_wide = jnp.repeat(value_rows, group_list, axis=1)
    scores = jnp.einsum('qhd,khd->hqk', queries, keys_wide, precision=lax.Precision.HIGHEST) * HEAD_SIZE ** (-0.5)
    allowed = (segment[:, None] == segment[None, :]) & (position[None, :] <= position[:, None])
    scores = low_back(jnp.where(allowed[None], scores, -1e+30))
    probabilities = lower_precision(jax.nn.softmax(scores, axis=-1))
    return jnp.einsum('hqk,khd->qhd', probabilities, values_wide, precision=lax.Precision.HIGHEST)

def layer(tokens_in, weights, segment, position):
    attn_gain, mlp_gain, q_scale, k_scale, w_qkv, w_hgate, w_out, w_gate, w_up, w_down = weights
    count_of_rows = tokens_in.shape[0]
    blocks = count_of_rows // TOK_DEV
    normed = lower_precision(normalize(tokens_in, attn_gain))
    projected_rows = low_back(product(normed, w_qkv))
    logits = low_back(product(normed, w_hgate))

    def block_fn(packed):
        return attend(packed[0], packed[1], packed[2], q_scale, k_scale)
    head_out = lax.map(jax.checkpoint(block_fn), (projected_rows.reshape(blocks, TOK_DEV, -1), segment.reshape(blocks, TOK_DEV), position.reshape(blocks, TOK_DEV)))
    head_out = low_back(head_out.reshape(count_of_rows, QUERY_HEADS, HEAD_SIZE))
    gated = lower_precision(head_out * jax.nn.sigmoid(logits)[:, :, None]).reshape(count_of_rows, QUERY_HEADS * HEAD_SIZE)
    residual = tokens_in + low_back(product(gated, w_out.T))
    normed_two = lower_precision(normalize(residual, mlp_gain))
    gate_pre = low_back(product(normed_two, w_gate))
    up_pre = low_back(product(normed_two, w_up))
    hidden = lower_precision(jax.nn.silu(gate_pre) * up_pre)
    return residual + product(hidden, w_down.T)

def reference(tokens, cotangent, lengths, deal_order, attn_gain, mlp_gain, q_scale, k_scale, w_qkv, w_hgate, w_out, w_gate, w_up, w_down):
    params = tuple((weight.astype(jnp.float32) for weight in (attn_gain, mlp_gain, q_scale, k_scale, w_qkv, w_hgate, w_out, w_gate, w_up, w_down)))

    def one_group(totals, inputs):
        group_tokens, group_cot, group_lengths, group_order = inputs
        source, segment, position = deal_map(group_lengths, group_order)

        def forward(tokens_in, weights):
            return layer(tokens_in, weights, segment, position)
        result, pullback = jax.vjp(forward, group_tokens[source].astype(jnp.float32), params)
        grad_tokens, grad_params = pullback(group_cot[source].astype(jnp.float32))
        placed_out = jnp.zeros(result.shape, jnp.float32).at[source].set(result).astype(jnp.bfloat16)
        placed_grad = jnp.zeros(result.shape, jnp.float32).at[source].set(grad_tokens).astype(jnp.bfloat16)
        totals = tuple((running + grad_part for running, grad_part in zip(totals, grad_params)))
        return (totals, (placed_out, placed_grad))
    initial = tuple((jnp.zeros(weight.shape, jnp.float32) for weight in params))
    sums, (outputs, token_grads) = lax.scan(one_group, initial, (tokens, cotangent, lengths, deal_order))
    return (outputs, token_grads, sums[0], sums[1], sums[2], sums[3], sums[4], sums[5], sums[6], sums[7], sums[8], sums[9])
```

```python
import jax
import jax.numpy as jnp
from jax import lax
from jax.sharding import PartitionSpec as P

QUERY_HEADS = 16
KEY_VALUE_HEADS = 8
HEAD_SIZE = 128
FF = 6144


eps_norm = 1e-06
rope_base = 1000000.0


def matmul(left, right):
    return jnp.dot(left, right, preferred_element_type=jnp.float32)


def contract_rows(left, right):
    return lax.dot_general(
        left, right, (((0,), (0,)), ((), ())), preferred_element_type=jnp.float32
    )


def contract_cols(left, right):
    return lax.dot_general(
        left, right, (((1,), (1,)), ((), ())), preferred_element_type=jnp.float32
    )


def normalize(value_rows):
    factor = lax.rsqrt(jnp.mean(value_rows * value_rows, axis=-1, keepdims=True) + eps_norm)
    return (value_rows * factor, factor)


def norm_back(grad_normed, normed_unit, factor, gain):
    scaled = grad_normed * gain
    return factor * (scaled - normed_unit * jnp.mean(scaled * normed_unit, axis=-1, keepdims=True))


def rope_tables(positions):
    half_dim = HEAD_SIZE // 2
    frequency = jnp.power(rope_base, -2.0 * jnp.arange(half_dim, dtype=jnp.float32) / HEAD_SIZE)
    angles = positions.astype(jnp.float32)[:, None] * frequency[None, :]
    angles = jnp.concatenate([angles, angles], axis=1)
    return (jnp.cos(angles)[:, None, :], jnp.sin(angles)[:, None, :])


def rotate(value_rows, cosine, sine_table):
    half_dim = value_rows.shape[-1] // 2
    turned = jnp.concatenate([-value_rows[..., half_dim:], value_rows[..., :half_dim]], axis=-1)
    return value_rows * cosine + turned * sine_table


def unrotate(grads, cosine, sine_table):
    half_dim = grads.shape[-1] // 2
    shifted = grads * sine_table
    turned = jnp.concatenate([shifted[..., half_dim:], -shifted[..., :half_dim]], axis=-1)
    return grads * cosine + turned


LANES = 8
HALO = 64
BITS = (2, 4, 1)


def exchange(value, bit):
    count = lax.axis_size("rep")
    return lax.ppermute(value, "rep", [(i, i ^ bit) for i in range(count)])


def plane_gather(rows):
    for bit in BITS:
        rows = jnp.concatenate([rows, exchange(rows, bit)], axis=0)
    return rows


def plane_scatter(partial):
    for bit in reversed(BITS):
        half = partial.shape[0] // 2
        arrived = exchange(partial[half:].astype(jnp.bfloat16), bit)
        partial = partial[:half] + arrived.astype(jnp.float32)
    return partial


def plane_groups():
    count = lax.axis_size("rep")
    if count == LANES:
        return None
    return [list(range(first, first + LANES)) for first in range(0, count, LANES)]


def sum_owned(partial):
    total = lax.psum_scatter(
        partial.astype(jnp.bfloat16), "fsdp", scatter_dimension=0, tiled=True
    )
    bit = LANES
    while bit < lax.axis_size("rep"):
        total = (total.astype(jnp.float32) + exchange(total, bit).astype(jnp.float32)).astype(
            jnp.bfloat16
        )
        bit *= 2
    return total


def all_columns(owned):
    return lax.all_gather(owned, "rep", axis=0, axis_index_groups=plane_groups())


def side_by_side(blocks):
    lanes, rows, columns = blocks.shape
    return blocks.transpose(1, 0, 2).reshape(rows, lanes * columns).astype(jnp.float32)


def take_cols(weight, first, count):
    return lax.dynamic_slice_in_dim(weight, first, count, 1)


def on_device(
    tokens,
    cotangent,
    lengths,
    deal_order,
    attn_gain,
    mlp_gain,
    q_scale,
    k_scale,
    w_qkv,
    w_hgate,
    w_out,
    w_gate,
    w_up,
    w_down,
):
    f32, bf16 = jnp.float32, jnp.bfloat16
    rows = tokens.shape[1]
    width = tokens.shape[2]
    shards = lax.axis_size("fsdp")
    shard = lax.axis_index("fsdp")
    lane = lax.rem(lax.axis_index("rep"), LANES)
    group_list = QUERY_HEADS // KEY_VALUE_HEADS
    q_cols = group_list * HEAD_SIZE
    ff_cols = w_gate.shape[1] // LANES
    out_rows = w_out.shape[0]

    def padded(vector):
        return jnp.pad(vector, (0, out_rows - vector.shape[0]))[:, None]

    weights_one = jnp.concatenate(
        [
            take_cols(w_qkv, lane * q_cols, q_cols),
            take_cols(w_qkv, QUERY_HEADS * HEAD_SIZE + lane * HEAD_SIZE, HEAD_SIZE),
            take_cols(
                w_qkv, (QUERY_HEADS + KEY_VALUE_HEADS) * HEAD_SIZE + lane * HEAD_SIZE, HEAD_SIZE
            ),
            jnp.pad(
                jnp.concatenate(
                    [
                        take_cols(w_hgate, lane * group_list, group_list),
                        attn_gain[:, None],
                        mlp_gain[:, None],
                        padded(q_scale),
                        padded(k_scale),
                    ],
                    axis=1,
                ),
                ((0, 0), (0, 128 - group_list - 4)),
            ),
            take_cols(w_out, lane * q_cols, q_cols),
        ],
        axis=1,
    )
    weights_one = lax.all_gather(weights_one, "fsdp", axis=0, tiled=True)
    weights_two = lax.all_gather(
        jnp.concatenate(
            [take_cols(w_gate, lane * ff_cols, ff_cols), take_cols(w_up, lane * ff_cols, ff_cols)],
            axis=1,
        ),
        "fsdp",
        axis=0,
        tiled=True,
    )
    weights_three = lax.all_gather(
        take_cols(w_down, lane * ff_cols, ff_cols), "fsdp", axis=0, tiled=True
    )
    qkv_cols = q_cols + 2 * HEAD_SIZE
    w_in = weights_one[:, : qkv_cols + 128]
    w_attn = weights_one[:, qkv_cols + 128 :]
    extra = weights_one[:, qkv_cols : qkv_cols + group_list + 4].astype(f32)
    gain_one = extra[:, group_list]
    gain_two = extra[:, group_list + 1]
    scales = extra.reshape(shards, width // shards, group_list + 4)[:, : HEAD_SIZE // shards]
    query_gain = scales[:, :, group_list + 2].reshape(HEAD_SIZE)
    key_gain = scales[:, :, group_list + 3].reshape(HEAD_SIZE)

    seq_lengths = lengths[0]
    ends = jnp.cumsum(seq_lengths)
    starts = ends - seq_lengths
    own_index = shard * rows + jnp.arange(rows, dtype=jnp.int32)
    begun = own_index[:, None] >= starts[None, :]
    own_position = own_index - jnp.max(jnp.where(begun, starts[None, :], 0), axis=1)

    own_x = tokens[0]
    own_dy = cotangent[0]
    gathered = plane_gather(
        jnp.concatenate(
            [own_x, jnp.broadcast_to(own_position.astype(bf16)[:, None], (rows, 128))], axis=1
        )
    )
    stream_all = gathered[:, :width].astype(f32)
    position = gathered[:, width].astype(jnp.int32)
    cot_all = plane_gather(own_dy)
    total_rows = LANES * rows

    normed_one = (normalize(stream_all)[0] * gain_one).astype(bf16)
    projected = matmul(normed_one, w_in)
    head_logit = projected[:, qkv_cols : qkv_cols + group_list]
    query_raw = projected[:, :q_cols].reshape(total_rows, group_list, HEAD_SIZE)
    key_raw = projected[:, q_cols : q_cols + HEAD_SIZE].reshape(total_rows, 1, HEAD_SIZE)
    values = projected[:, q_cols + HEAD_SIZE : qkv_cols].astype(bf16)
    query_unit, query_factor = normalize(query_raw)
    key_unit, key_factor = normalize(key_raw)
    cosine, sine_table = rope_tables(position)
    queries = (
        rotate(query_unit * query_gain, cosine, sine_table)
        .astype(bf16)
        .reshape(LANES, rows, group_list, HEAD_SIZE)
        .transpose(0, 2, 1, 3)
        .reshape(LANES, group_list * rows, HEAD_SIZE)
    )
    keys = rotate(key_unit * key_gain, cosine, sine_table).astype(bf16)
    key_value = jnp.concatenate([keys.reshape(total_rows, HEAD_SIZE), values], axis=1).reshape(
        LANES, rows, 2 * HEAD_SIZE
    )
    before = lax.ppermute(
        key_value[:, rows - HALO :], "fsdp", [(i, i + 1) for i in range(shards - 1)]
    )
    key_value = jnp.concatenate([before, key_value], axis=1)
    keys_wide = key_value[:, :, :HEAD_SIZE]
    values_wide = key_value[:, :, HEAD_SIZE:]
    local = jnp.arange(rows, dtype=jnp.int32)
    offset = jnp.arange(HALO + rows, dtype=jnp.int32) - HALO
    allowed = (offset[None, None, :] <= local[None, :, None]) & (
        offset[None, None, :] >= local[None, :, None] - position.reshape(LANES, rows)[:, :, None]
    )
    scores = jnp.einsum(
        "sqd,spd->sqp", queries, keys_wide, preferred_element_type=f32
    ) * HEAD_SIZE ** (-0.5)
    scores = jnp.where(jnp.concatenate([allowed] * group_list, axis=1), scores, -1e30)
    weights_exp = jnp.exp(scores - jnp.max(scores, axis=-1, keepdims=True))
    probs = weights_exp / jnp.sum(weights_exp, axis=-1, keepdims=True)
    probs_low = probs.astype(bf16)

    def by_row(value):
        return (
            value.reshape(LANES, group_list, rows, HEAD_SIZE)
            .transpose(0, 2, 1, 3)
            .reshape(total_rows, group_list, HEAD_SIZE)
        )

    def by_head(value):
        return (
            value.reshape(LANES, rows, group_list, HEAD_SIZE)
            .transpose(0, 2, 1, 3)
            .reshape(LANES, group_list * rows, HEAD_SIZE)
        )

    head_out = by_row(
        jnp.einsum("sqp,spd->sqd", probs_low, values_wide, preferred_element_type=f32)
    )
    head_gate = jax.nn.sigmoid(head_logit)
    gated = (head_out * head_gate[:, :, None]).astype(bf16).reshape(total_rows, q_cols)
    residual = own_x.astype(f32) + plane_scatter(contract_cols(gated, w_attn))
    unit_two, factor_two = normalize(residual)
    normed_two = plane_gather((unit_two * gain_two).astype(bf16))
    pre = matmul(normed_two, weights_two)
    gate_pre = pre[:, :ff_cols]
    up_pre = pre[:, ff_cols:]
    gate_sig = jax.nn.sigmoid(gate_pre)
    gate_act = gate_pre * gate_sig
    hidden = (gate_act * up_pre).astype(bf16)
    down_sum = sum_owned(contract_rows(cot_all, hidden))
    final_rows = residual + plane_scatter(contract_cols(hidden, weights_three))

    grad_hidden = matmul(cot_all, weights_three)
    grad_pre = jnp.concatenate(
        [
            (grad_hidden * up_pre * gate_sig * (1.0 + gate_pre * (1.0 - gate_sig))).astype(bf16),
            (grad_hidden * gate_act).astype(bf16),
        ],
        axis=1,
    )
    pre_sum = sum_owned(contract_rows(normed_two, grad_pre))
    contribution = plane_scatter(contract_cols(grad_pre, weights_two))
    grad_gain_two = jnp.sum(contribution * unit_two, axis=0)
    grad_resid = own_dy.astype(f32) + norm_back(contribution, unit_two, factor_two, gain_two)
    grad_branch = plane_gather(grad_resid.astype(bf16))
    grad_gated = matmul(grad_branch, w_attn).reshape(total_rows, group_list, HEAD_SIZE)
    grad_heads = by_head((grad_gated * head_gate[:, :, None]).astype(bf16))
    grad_logit = (jnp.sum(grad_gated * head_out, axis=-1) * head_gate * (1.0 - head_gate)).astype(
        bf16
    )
    grad_probs = jnp.einsum("sqd,spd->sqp", grad_heads, values_wide, preferred_element_type=f32)
    grad_values = jnp.einsum("sqp,sqd->spd", probs_low, grad_heads, preferred_element_type=f32)
    grad_scores = (
        probs * (grad_probs - jnp.sum(probs * grad_probs, axis=-1, keepdims=True))
    ).astype(bf16)
    grad_queries = (
        jnp.einsum("sqp,spd->sqd", grad_scores, keys_wide, preferred_element_type=f32)
        * HEAD_SIZE ** (-0.5)
    ).astype(bf16)
    grad_keys = jnp.einsum("sqp,sqd->spd", grad_scores, queries, preferred_element_type=f32)
    grad_key_value = jnp.concatenate([grad_keys, grad_values], axis=2)
    after = lax.ppermute(
        grad_key_value[:, :HALO].astype(bf16), "fsdp", [(i + 1, i) for i in range(shards - 1)]
    )
    grad_key_value = grad_key_value[:, HALO:] + jnp.pad(
        after.astype(f32), ((0, 0), (rows - HALO, 0), (0, 0))
    )
    grad_keys = (grad_key_value[:, :, :HEAD_SIZE] * HEAD_SIZE ** (-0.5)).astype(bf16)
    grad_values = grad_key_value[:, :, HEAD_SIZE:].reshape(total_rows, HEAD_SIZE)
    grad_query_rot = unrotate(by_row(grad_queries).astype(f32), cosine, sine_table)
    grad_key_rot = unrotate(
        grad_keys.astype(f32).reshape(total_rows, 1, HEAD_SIZE), cosine, sine_table
    )
    grad_query_gain = jnp.sum(grad_query_rot * query_unit, axis=(0, 1))
    grad_key_gain = jnp.sum(grad_key_rot * key_unit, axis=(0, 1))
    grad_query_raw = norm_back(grad_query_rot, query_unit, query_factor, query_gain)
    grad_key_raw = norm_back(grad_key_rot, key_unit, key_factor, key_gain)
    grad_projected = jnp.concatenate(
        [
            grad_query_raw.reshape(total_rows, q_cols),
            grad_key_raw.reshape(total_rows, HEAD_SIZE),
            grad_values,
            jnp.pad(grad_logit.astype(f32), ((0, 0), (0, 128 - group_list))),
        ],
        axis=1,
    ).astype(bf16)

    grad_normed_one = plane_scatter(contract_cols(grad_projected, w_in))
    grad_in = contract_rows(normed_one, grad_projected)
    attn_sum = sum_owned(
        jnp.concatenate([grad_in[:, :qkv_cols], contract_rows(grad_branch, gated)], axis=1)
    )
    unit_one, factor_one = normalize(own_x.astype(f32))
    grad_gain_one = jnp.sum(grad_normed_one * unit_one, axis=0)
    grad_stream = grad_resid + norm_back(grad_normed_one, unit_one, factor_one, gain_one)

    lane_mask = (jnp.arange(LANES) == lane).astype(f32)
    grad_hgate = grad_in[:, qkv_cols : qkv_cols + group_list].T
    small = jnp.concatenate(
        [
            (lane_mask[:, None, None] * grad_hgate[None]).reshape(QUERY_HEADS, width),
            grad_gain_one[None],
            grad_gain_two[None],
            jnp.pad(grad_query_gain, (0, width - HEAD_SIZE))[None],
            jnp.pad(grad_key_gain, (0, width - HEAD_SIZE))[None],
            jnp.zeros((4, width), f32),
        ],
        axis=0,
    )
    small = lax.psum(small, ("fsdp", "rep"))

    def own_part(vector):
        piece = vector.shape[-1] // shards
        return lax.dynamic_slice_in_dim(vector, shard * piece, piece, vector.ndim - 1)

    down_all = all_columns(down_sum)
    pre_all = all_columns(pre_sum)
    attn_all = all_columns(attn_sum)
    return (
        final_rows.astype(bf16)[None],
        grad_stream.astype(bf16)[None],
        own_part(small[QUERY_HEADS]),
        own_part(small[QUERY_HEADS + 1]),
        own_part(small[QUERY_HEADS + 2, :HEAD_SIZE]),
        own_part(small[QUERY_HEADS + 3, :HEAD_SIZE]),
        jnp.concatenate(
            [
                side_by_side(attn_all[:, :, :q_cols]),
                side_by_side(attn_all[:, :, q_cols : q_cols + HEAD_SIZE]),
                side_by_side(attn_all[:, :, q_cols + HEAD_SIZE : qkv_cols]),
            ],
            axis=1,
        ),
        own_part(small[:QUERY_HEADS]).T,
        side_by_side(attn_all[:, :, qkv_cols:]),
        side_by_side(pre_all[:, :, :ff_cols]),
        side_by_side(pre_all[:, :, ff_cols:]),
        side_by_side(down_all),
    )


def solution(mesh):
    return jax.shard_map(
        on_device,
        mesh=mesh,
        in_specs=(
            P("rep", "fsdp", None),
            P("rep", "fsdp", None),
            P("rep", None),
            P("rep", None),
            P("fsdp"),
            P("fsdp"),
            P("fsdp"),
            P("fsdp"),
            P("fsdp", None),
            P("fsdp", None),
            P("fsdp", None),
            P("fsdp", None),
            P("fsdp", None),
            P("fsdp", None),
        ),
        out_specs=(
            P("rep", "fsdp", None),
            P("rep", "fsdp", None),
            P("fsdp"),
            P("fsdp"),
            P("fsdp"),
            P("fsdp"),
            P("fsdp", None),
            P("fsdp", None),
            P("fsdp", None),
            P("fsdp", None),
            P("fsdp", None),
            P("fsdp", None),
        ),
        check_vma=False,
    )
```

```python
import jax
import jax.numpy as jnp
from jax import lax
from jax.experimental import pallas as pl
from jax.experimental.pallas import tpu as pltpu
from jax.sharding import PartitionSpec as P

QUERY_HEADS = 16
KEY_VALUE_HEADS = 8
HEAD_SIZE = 128
FF = 6144


eps_norm = 1e-06
rope_base = 1000000.0


def matmul(left, right):
    return jnp.dot(left, right, preferred_element_type=jnp.float32)


def contract_rows(left, right):
    return lax.dot_general(
        left, right, (((0,), (0,)), ((), ())), preferred_element_type=jnp.float32
    )


def contract_cols(left, right):
    return lax.dot_general(
        left, right, (((1,), (1,)), ((), ())), preferred_element_type=jnp.float32
    )


def normalize(value_rows):
    factor = lax.rsqrt(jnp.mean(value_rows * value_rows, axis=-1, keepdims=True) + eps_norm)
    return (value_rows * factor, factor)


def norm_back(grad_normed, normed_unit, factor, gain):
    scaled = grad_normed * gain
    return factor * (scaled - normed_unit * jnp.mean(scaled * normed_unit, axis=-1, keepdims=True))


def rope_tables(positions):
    half_dim = HEAD_SIZE // 2
    frequency = jnp.power(rope_base, -2.0 * jnp.arange(half_dim, dtype=jnp.float32) / HEAD_SIZE)
    angles = positions.astype(jnp.float32)[:, None] * frequency[None, :]
    angles = jnp.concatenate([angles, angles], axis=1)
    return (jnp.cos(angles)[:, None, :], jnp.sin(angles)[:, None, :])


def rotate(value_rows, cosine, sine_table):
    half_dim = value_rows.shape[-1] // 2
    turned = jnp.concatenate([-value_rows[..., half_dim:], value_rows[..., :half_dim]], axis=-1)
    return value_rows * cosine + turned * sine_table


def unrotate(grads, cosine, sine_table):
    half_dim = grads.shape[-1] // 2
    shifted = grads * sine_table
    turned = jnp.concatenate([shifted[..., half_dim:], -shifted[..., :half_dim]], axis=-1)
    return grads * cosine + turned


LANES = 8
HALO = 64


def exchange(value, bit):
    count = lax.axis_size("rep")
    return lax.ppermute(value, "rep", [(i, i ^ bit) for i in range(count)])


def plane_slots(rows):
    half = rows.shape[1] // 256 * 128
    near, far = exchange(rows, 2), exchange(rows, 4)
    corner = jnp.concatenate([exchange(far[:, :half], 2), exchange(near[:, half:], 4)], axis=1)
    slots = []
    for piece in (rows, near, far, corner):
        slots += [piece, exchange(piece, 1)]
    return slots


def plane_gather(rows):
    return jnp.concatenate(plane_slots(rows), axis=0)


def plane_scatter(partial):
    slots = partial.reshape(LANES, partial.shape[0] // LANES, partial.shape[1])
    half = partial.shape[1] // 2

    def sent(value, bit):
        return exchange(value.astype(jnp.bfloat16), bit).astype(jnp.float32)

    corner, far, near, own = (slots[k] + sent(slots[k + 1], 1) for k in (6, 4, 2, 0))
    far_left = far[:, :half] + sent(corner[:, :half], 2)
    near_right = near[:, half:] + sent(corner[:, half:], 4)
    return (
        own
        + jnp.concatenate([sent(near[:, :half], 2), sent(near_right, 2)], axis=1)
        + jnp.concatenate([sent(far_left, 4), sent(far[:, half:], 4)], axis=1)
    )


class OwnedSum:
    def __init__(self, partial):
        self.count = lax.axis_size("fsdp")
        self.me = lax.axis_index("fsdp")
        self.partial = partial.astype(jnp.bfloat16)
        self.moved = ()
        self.done = 0

    def rows_of(self, owner):
        piece = self.partial.shape[0] // self.count
        owner = jnp.clip(owner, 0, self.count - 1)
        return lax.dynamic_slice_in_dim(self.partial, owner * piece, piece, 0)

    def added(self, *values):
        total = values[0].astype(jnp.float32)
        for value in values[1:]:
            total = total + value.astype(jnp.float32)
        return total.astype(jnp.bfloat16)

    def step(self):
        self.done += 1
        far = self.count - self.done
        rise = (self.rows_of(self.me + far),) + self.moved[:1]
        fall = (self.rows_of(self.me - far),) + self.moved[1:]
        self.moved = (
            lax.ppermute(self.added(*rise), "fsdp", [(i, i + 1) for i in range(self.done)]),
            lax.ppermute(
                self.added(*fall), "fsdp", [(i, i - 1) for i in range(far, self.count)]
            ),
        )

    def before(self, *values):
        tied = lax.optimization_barrier((*values, *self.moved))
        self.moved = tied[len(values) :]
        return tied[0] if len(values) == 1 else tied[: len(values)]

    def total(self):
        while self.done < self.count - 1:
            self.step()
        total = self.added(self.rows_of(self.me), *self.moved)
        bit = LANES
        while bit < lax.axis_size("rep"):
            total = self.added(total, exchange(total, bit))
            bit *= 2
        return total


def lay_out(lane, slots, splits):
    rows, columns = slots[0].shape
    tile = 64

    def kernel(lane_ref, *refs):
        for slot in range(LANES):
            owner = lane_ref[0] ^ slot
            for parts, out in zip(splits, refs[LANES:]):
                base = 0
                for start, count in parts:
                    place = pl.ds(pl.multiple_of(base + owner * count, 128), count)
                    out[:, place] = refs[slot][:, start : start + count].astype(jnp.float32)
                    base += LANES * count

    totals = [LANES * sum(count for _, count in parts) for parts in splits]
    return pl.pallas_call(
        kernel,
        grid_spec=pltpu.PrefetchScalarGridSpec(
            num_scalar_prefetch=1,
            grid=(rows // tile,),
            in_specs=[pl.BlockSpec((tile, columns), lambda i, _: (i, 0))] * LANES,
            out_specs=[pl.BlockSpec((tile, total), lambda i, _: (i, 0)) for total in totals],
        ),
        out_shape=[jax.ShapeDtypeStruct((rows, total), jnp.float32) for total in totals],
        cost_estimate=pl.CostEstimate(
            flops=0, transcendentals=0, bytes_accessed=6 * LANES * rows * columns
        ),
    )(lane.reshape(1), *slots)


def take_cols(weight, first, count):
    return lax.dynamic_slice_in_dim(weight, first, count, 1)


def on_device(
    tokens,
    cotangent,
    lengths,
    deal_order,
    attn_gain,
    mlp_gain,
    q_scale,
    k_scale,
    w_qkv,
    w_hgate,
    w_out,
    w_gate,
    w_up,
    w_down,
):
    f32, bf16 = jnp.float32, jnp.bfloat16
    rows = tokens.shape[1]
    width = tokens.shape[2]
    shards = lax.axis_size("fsdp")
    shard = lax.axis_index("fsdp")
    lane = lax.rem(lax.axis_index("rep"), LANES)
    group_list = QUERY_HEADS // KEY_VALUE_HEADS
    q_cols = group_list * HEAD_SIZE
    ff_cols = w_gate.shape[1] // LANES
    out_rows = w_out.shape[0]

    def padded(vector):
        return jnp.pad(vector, (0, out_rows - vector.shape[0]))[:, None]

    weights_one = jnp.concatenate(
        [
            take_cols(w_qkv, lane * q_cols, q_cols),
            take_cols(w_qkv, QUERY_HEADS * HEAD_SIZE + lane * HEAD_SIZE, HEAD_SIZE),
            take_cols(
                w_qkv, (QUERY_HEADS + KEY_VALUE_HEADS) * HEAD_SIZE + lane * HEAD_SIZE, HEAD_SIZE
            ),
            jnp.pad(
                jnp.concatenate(
                    [
                        take_cols(w_hgate, lane * group_list, group_list),
                        attn_gain[:, None],
                        mlp_gain[:, None],
                        padded(q_scale),
                        padded(k_scale),
                    ],
                    axis=1,
                ),
                ((0, 0), (0, 128 - group_list - 4)),
            ),
            take_cols(w_out, lane * q_cols, q_cols),
        ],
        axis=1,
    )
    weights_one = lax.all_gather(weights_one, "fsdp", axis=0, tiled=True)
    weights_two = lax.all_gather(
        jnp.concatenate(
            [take_cols(w_gate, lane * ff_cols, ff_cols), take_cols(w_up, lane * ff_cols, ff_cols)],
            axis=1,
        ),
        "fsdp",
        axis=0,
        tiled=True,
    )
    weights_three = lax.all_gather(
        take_cols(w_down, lane * ff_cols, ff_cols), "fsdp", axis=0, tiled=True
    )
    qkv_cols = q_cols + 2 * HEAD_SIZE
    w_in = weights_one[:, : qkv_cols + 128]
    w_attn = weights_one[:, qkv_cols + 128 :]
    extra = weights_one[:, qkv_cols : qkv_cols + group_list + 4].astype(f32)
    gain_one = extra[:, group_list]
    gain_two = extra[:, group_list + 1]
    scales = extra.reshape(shards, width // shards, group_list + 4)[:, : HEAD_SIZE // shards]
    query_gain = scales[:, :, group_list + 2].reshape(HEAD_SIZE)
    key_gain = scales[:, :, group_list + 3].reshape(HEAD_SIZE)

    seq_lengths = lengths[0]
    ends = jnp.cumsum(seq_lengths)
    starts = ends - seq_lengths
    own_index = shard * rows + jnp.arange(rows, dtype=jnp.int32)
    begun = own_index[:, None] >= starts[None, :]
    own_position = own_index - jnp.max(jnp.where(begun, starts[None, :], 0), axis=1)

    own_x = tokens[0]
    own_dy = cotangent[0]
    gathered = plane_gather(
        jnp.concatenate(
            [own_x, jnp.broadcast_to(own_position.astype(bf16)[:, None], (rows, 128))], axis=1
        )
    )
    stream_all = gathered[:, :width].astype(f32)
    position = gathered[:, width].astype(jnp.int32)
    cot_all = plane_gather(own_dy)
    total_rows = LANES * rows

    normed_one = (normalize(stream_all)[0] * gain_one).astype(bf16)
    projected = matmul(normed_one, w_in)
    head_logit = projected[:, qkv_cols : qkv_cols + group_list]
    query_raw = projected[:, :q_cols].reshape(total_rows, group_list, HEAD_SIZE)
    key_raw = projected[:, q_cols : q_cols + HEAD_SIZE].reshape(total_rows, 1, HEAD_SIZE)
    values = projected[:, q_cols + HEAD_SIZE : qkv_cols].astype(bf16)
    query_unit, query_factor = normalize(query_raw)
    key_unit, key_factor = normalize(key_raw)
    cosine, sine_table = rope_tables(position)
    queries = (
        rotate(query_unit * query_gain, cosine, sine_table)
        .astype(bf16)
        .reshape(LANES, rows, group_list, HEAD_SIZE)
        .transpose(0, 2, 1, 3)
        .reshape(LANES, group_list * rows, HEAD_SIZE)
    )
    keys = rotate(key_unit * key_gain, cosine, sine_table).astype(bf16)
    key_value = jnp.concatenate([keys.reshape(total_rows, HEAD_SIZE), values], axis=1).reshape(
        LANES, rows, 2 * HEAD_SIZE
    )
    before = lax.ppermute(
        key_value[:, rows - HALO :], "fsdp", [(i, i + 1) for i in range(shards - 1)]
    )
    key_value = jnp.concatenate([before, key_value], axis=1)
    keys_wide = key_value[:, :, :HEAD_SIZE]
    values_wide = key_value[:, :, HEAD_SIZE:]
    local = jnp.arange(rows, dtype=jnp.int32)
    offset = jnp.arange(HALO + rows, dtype=jnp.int32) - HALO
    allowed = (offset[None, None, :] <= local[None, :, None]) & (
        offset[None, None, :] >= local[None, :, None] - position.reshape(LANES, rows)[:, :, None]
    )
    scores = jnp.einsum(
        "sqd,spd->sqp", queries, keys_wide, preferred_element_type=f32
    ) * HEAD_SIZE ** (-0.5)
    scores = jnp.where(jnp.concatenate([allowed] * group_list, axis=1), scores, -1e30)
    weights_exp = jnp.exp(scores - jnp.max(scores, axis=-1, keepdims=True))
    probs = weights_exp / jnp.sum(weights_exp, axis=-1, keepdims=True)
    probs_low = probs.astype(bf16)

    def by_row(value):
        return (
            value.reshape(LANES, group_list, rows, HEAD_SIZE)
            .transpose(0, 2, 1, 3)
            .reshape(total_rows, group_list, HEAD_SIZE)
        )

    def by_head(value):
        return (
            value.reshape(LANES, rows, group_list, HEAD_SIZE)
            .transpose(0, 2, 1, 3)
            .reshape(LANES, group_list * rows, HEAD_SIZE)
        )

    head_out = by_row(
        jnp.einsum("sqp,spd->sqd", probs_low, values_wide, preferred_element_type=f32)
    )
    head_gate = jax.nn.sigmoid(head_logit)
    gated = (head_out * head_gate[:, :, None]).astype(bf16).reshape(total_rows, q_cols)
    residual = own_x.astype(f32) + plane_scatter(contract_cols(gated, w_attn))
    unit_two, factor_two = normalize(residual)
    normed_two = plane_gather((unit_two * gain_two).astype(bf16))
    pre = matmul(normed_two, weights_two)
    gate_pre = pre[:, :ff_cols]
    up_pre = pre[:, ff_cols:]
    gate_sig = jax.nn.sigmoid(gate_pre)
    gate_act = gate_pre * gate_sig
    hidden = (gate_act * up_pre).astype(bf16)
    down_sum = OwnedSum(contract_rows(cot_all, hidden))
    down_sum.step()
    weights_three = down_sum.before(weights_three)

    grad_hidden = matmul(cot_all, weights_three)
    grad_pre = jnp.concatenate(
        [
            (grad_hidden * up_pre * gate_sig * (1.0 + gate_pre * (1.0 - gate_sig))).astype(bf16),
            (grad_hidden * gate_act).astype(bf16),
        ],
        axis=1,
    )
    grad_pre = down_sum.before(grad_pre)
    down_sum.step()
    pre_sum = OwnedSum(contract_rows(normed_two, grad_pre))
    grad_pre, pre_sum.partial = lax.optimization_barrier((grad_pre, pre_sum.partial))
    pre_sum.step()
    contribution = plane_scatter(contract_cols(grad_pre, weights_two))
    grad_gain_two = jnp.sum(contribution * unit_two, axis=0)
    grad_resid = own_dy.astype(f32) + norm_back(contribution, unit_two, factor_two, gain_two)
    down_sum = down_sum.total()
    grad_branch, down_sum = pre_sum.before(grad_resid.astype(bf16), down_sum)
    down_all = plane_slots(down_sum)
    for _ in range(shards - 3):
        pre_sum.step()
    grad_branch = pre_sum.before(plane_gather(grad_branch))
    grad_branch, hidden = lax.optimization_barrier((grad_branch, hidden))
    final_rows = residual + plane_scatter(contract_cols(hidden, weights_three))
    final_rows = final_rows.astype(bf16)
    pre_sum = pre_sum.total()
    pre_all = plane_slots(pre_sum)
    out_sum = OwnedSum(contract_rows(grad_branch, gated)).total()
    grad_gated = matmul(grad_branch, w_attn).reshape(total_rows, group_list, HEAD_SIZE)
    grad_heads = by_head((grad_gated * head_gate[:, :, None]).astype(bf16))
    grad_logit = (jnp.sum(grad_gated * head_out, axis=-1) * head_gate * (1.0 - head_gate)).astype(
        bf16
    )
    grad_probs = jnp.einsum("sqd,spd->sqp", grad_heads, values_wide, preferred_element_type=f32)
    grad_values = jnp.einsum("sqp,sqd->spd", probs_low, grad_heads, preferred_element_type=f32)
    grad_scores = (
        probs * (grad_probs - jnp.sum(probs * grad_probs, axis=-1, keepdims=True))
    ).astype(bf16)
    grad_queries = (
        jnp.einsum("sqp,spd->sqd", grad_scores, keys_wide, preferred_element_type=f32)
        * HEAD_SIZE ** (-0.5)
    ).astype(bf16)
    grad_keys = jnp.einsum("sqp,sqd->spd", grad_scores, queries, preferred_element_type=f32)
    grad_key_value = jnp.concatenate([grad_keys, grad_values], axis=2)
    after = lax.ppermute(
        grad_key_value[:, :HALO].astype(bf16), "fsdp", [(i + 1, i) for i in range(shards - 1)]
    )
    grad_key_value = grad_key_value[:, HALO:] + jnp.pad(
        after.astype(f32), ((0, 0), (rows - HALO, 0), (0, 0))
    )
    grad_keys = (grad_key_value[:, :, :HEAD_SIZE] * HEAD_SIZE ** (-0.5)).astype(bf16)
    grad_values = grad_key_value[:, :, HEAD_SIZE:].reshape(total_rows, HEAD_SIZE)
    grad_query_rot = unrotate(by_row(grad_queries).astype(f32), cosine, sine_table)
    grad_key_rot = unrotate(
        grad_keys.astype(f32).reshape(total_rows, 1, HEAD_SIZE), cosine, sine_table
    )
    grad_query_gain = jnp.sum(grad_query_rot * query_unit, axis=(0, 1))
    grad_key_gain = jnp.sum(grad_key_rot * key_unit, axis=(0, 1))
    grad_query_raw = norm_back(grad_query_rot, query_unit, query_factor, query_gain)
    grad_key_raw = norm_back(grad_key_rot, key_unit, key_factor, key_gain)
    grad_projected = jnp.concatenate(
        [
            grad_query_raw.reshape(total_rows, q_cols),
            grad_key_raw.reshape(total_rows, HEAD_SIZE),
            grad_values,
            jnp.pad(grad_logit.astype(f32), ((0, 0), (0, 128 - group_list))),
        ],
        axis=1,
    ).astype(bf16)

    grad_projected, out_sum, final_rows = lax.optimization_barrier(
        (grad_projected, out_sum, final_rows)
    )
    out_all = plane_slots(out_sum)
    (w_down_grad,) = lay_out(lane, down_all, (((0, ff_cols),),))
    w_gate_grad, w_up_grad = lay_out(lane, pre_all, (((0, ff_cols),), ((ff_cols, ff_cols),)))
    (w_out_grad,) = lay_out(lane, out_all, (((0, q_cols),),))
    grad_normed_one = plane_scatter(contract_cols(grad_projected, w_in))
    grad_in = contract_rows(normed_one, grad_projected)
    unit_one, factor_one = normalize(own_x.astype(f32))
    grad_gain_one = jnp.sum(grad_normed_one * unit_one, axis=0)
    grad_stream = grad_resid + norm_back(grad_normed_one, unit_one, factor_one, gain_one)

    scale_rows = width // shards

    def scale_column(vector):
        vector = vector.reshape(shards, HEAD_SIZE // shards)
        return jnp.pad(vector, ((0, 0), (0, scale_rows - HEAD_SIZE // shards))).reshape(width)

    extra_grads = jnp.stack(
        [grad_gain_one, grad_gain_two, scale_column(grad_query_gain), scale_column(grad_key_gain)]
    )
    places = jnp.arange(128)[None, :] == group_list + jnp.arange(4)[:, None]
    extra_grads = contract_rows(extra_grads.astype(bf16), places.astype(bf16))
    in_sum = OwnedSum(grad_in + jnp.pad(extra_grads, ((0, 0), (qkv_cols, 0)))).total()
    in_all = plane_slots(in_sum)
    (w_qkv_grad,) = lay_out(
        lane, in_all, (((0, q_cols), (q_cols, HEAD_SIZE), (q_cols + HEAD_SIZE, HEAD_SIZE)),)
    )
    small = jnp.stack([slot[:, qkv_cols:] for slot in in_all]).astype(f32)
    by_owner = [lax.dynamic_index_in_dim(small, lane ^ k, 0, False) for k in range(LANES)]
    sums = jnp.sum(small[:, :, group_list : group_list + 4], axis=0)
    return (
        final_rows[None],
        grad_stream.astype(bf16)[None],
        sums[:, 0],
        sums[:, 1],
        sums[: HEAD_SIZE // shards, 2],
        sums[: HEAD_SIZE // shards, 3],
        w_qkv_grad,
        jnp.concatenate([block[:, :group_list] for block in by_owner], axis=1),
        w_out_grad,
        w_gate_grad,
        w_up_grad,
        w_down_grad,
    )


def solution(mesh):
    return jax.shard_map(
        on_device,
        mesh=mesh,
        in_specs=(
            P("rep", "fsdp", None),
            P("rep", "fsdp", None),
            P("rep", None),
            P("rep", None),
            P("fsdp"),
            P("fsdp"),
            P("fsdp"),
            P("fsdp"),
            P("fsdp", None),
            P("fsdp", None),
            P("fsdp", None),
            P("fsdp", None),
            P("fsdp", None),
            P("fsdp", None),
        ),
        out_specs=(
            P("rep", "fsdp", None),
            P("rep", "fsdp", None),
            P("fsdp"),
            P("fsdp"),
            P("fsdp"),
            P("fsdp"),
            P("fsdp", None),
            P("fsdp", None),
            P("fsdp", None),
            P("fsdp", None),
            P("fsdp", None),
            P("fsdp", None),
        ),
        check_vma=False,
    )
```

```python
import jax
import jax.numpy as jnp
from jax import lax
from jax.experimental import pallas as pl
from jax.experimental.pallas import tpu as pltpu
from jax.sharding import PartitionSpec as P

QUERY_HEADS = 16
KEY_VALUE_HEADS = 8
HEAD_SIZE = 128
FF = 6144


eps_norm = 1e-06
rope_base = 1000000.0


def matmul(left, right):
    return jnp.dot(left, right, preferred_element_type=jnp.float32)


def contract_rows(left, right):
    return lax.dot_general(
        left, right, (((0,), (0,)), ((), ())), preferred_element_type=jnp.float32
    )


def contract_cols(left, right):
    return lax.dot_general(
        left, right, (((1,), (1,)), ((), ())), preferred_element_type=jnp.float32
    )


def normalize(value_rows):
    factor = lax.rsqrt(jnp.mean(value_rows * value_rows, axis=-1, keepdims=True) + eps_norm)
    return (value_rows * factor, factor)


def norm_back(grad_normed, normed_unit, factor, gain):
    scaled = grad_normed * gain
    return factor * (scaled - normed_unit * jnp.mean(scaled * normed_unit, axis=-1, keepdims=True))


def rope_tables(positions):
    half_dim = HEAD_SIZE // 2
    frequency = jnp.power(rope_base, -2.0 * jnp.arange(half_dim, dtype=jnp.float32) / HEAD_SIZE)
    angles = positions.astype(jnp.float32)[:, None] * frequency[None, :]
    angles = jnp.concatenate([angles, angles], axis=1)
    return (jnp.cos(angles)[:, None, :], jnp.sin(angles)[:, None, :])


def rotate(value_rows, cosine, sine_table):
    half_dim = value_rows.shape[-1] // 2
    turned = jnp.concatenate([-value_rows[..., half_dim:], value_rows[..., :half_dim]], axis=-1)
    return value_rows * cosine + turned * sine_table


def unrotate(grads, cosine, sine_table):
    half_dim = grads.shape[-1] // 2
    shifted = grads * sine_table
    turned = jnp.concatenate([shifted[..., half_dim:], -shifted[..., :half_dim]], axis=-1)
    return grads * cosine + turned


LANES = 8
HALO = 64


def exchange(value, bit):
    count = lax.axis_size("rep")
    return lax.ppermute(value, "rep", [(i, i ^ bit) for i in range(count)])


def plane_slots(rows):
    half = rows.shape[1] // 256 * 128
    near, far = exchange(rows, 2), exchange(rows, 4)
    corner = jnp.concatenate([exchange(far[:, :half], 2), exchange(near[:, half:], 4)], axis=1)
    slots = []
    for piece in (rows, near, far, corner):
        slots += [piece, exchange(piece, 1)]
    return slots


def plane_gather(rows):
    return jnp.concatenate(plane_slots(rows), axis=0)


def plane_scatter(partial):
    slots = partial.reshape(LANES, partial.shape[0] // LANES, partial.shape[1])
    half = partial.shape[1] // 2

    def sent(value, bit):
        return exchange(value.astype(jnp.bfloat16), bit).astype(jnp.float32)

    corner, far, near, own = (slots[k] + sent(slots[k + 1], 1) for k in (6, 4, 2, 0))
    far_left = far[:, :half] + sent(corner[:, :half], 2)
    near_right = near[:, half:] + sent(corner[:, half:], 4)
    return (
        own
        + jnp.concatenate([sent(near[:, :half], 2), sent(near_right, 2)], axis=1)
        + jnp.concatenate([sent(far_left, 4), sent(far[:, half:], 4)], axis=1)
    )


class OwnedSum:
    def __init__(self, partial):
        self.count = lax.axis_size("fsdp")
        self.me = lax.axis_index("fsdp")
        self.partial = partial.astype(jnp.bfloat16)
        self.moved = ()
        self.done = 0

    def rows_of(self, owner):
        piece = self.partial.shape[0] // self.count
        owner = jnp.clip(owner, 0, self.count - 1)
        return lax.dynamic_slice_in_dim(self.partial, owner * piece, piece, 0)

    def added(self, *values):
        total = values[0].astype(jnp.float32)
        for value in values[1:]:
            total = total + value.astype(jnp.float32)
        return total.astype(jnp.bfloat16)

    def step(self, value=None):
        self.done += 1
        far = self.count - self.done
        rise = (self.rows_of(self.me + far),) + self.moved[:1]
        fall = (self.rows_of(self.me - far),) + self.moved[1:]
        rise, fall = self.added(*rise), self.added(*fall)
        if value is not None:
            rise, fall, value = lax.optimization_barrier((rise, fall, value))
        self.moved = (
            lax.ppermute(rise, "fsdp", [(i, i + 1) for i in range(self.done)]),
            lax.ppermute(fall, "fsdp", [(i, i - 1) for i in range(far, self.count)]),
        )
        return value

    def before(self, *values):
        tied = lax.optimization_barrier((*values, *self.moved))
        self.moved = tied[len(values) :]
        return tied[0] if len(values) == 1 else tied[: len(values)]

    def total(self):
        while self.done < self.count - 1:
            self.step()
        total = self.added(self.rows_of(self.me), *self.moved)
        bit = LANES
        while bit < lax.axis_size("rep"):
            total = self.added(total, exchange(total, bit))
            bit *= 2
        return total


def lay_out(lane, slots, splits):
    rows, columns = slots[0].shape
    tile = 64

    def kernel(lane_ref, *refs):
        for slot in range(LANES):
            owner = lane_ref[0] ^ slot
            for parts, out in zip(splits, refs[LANES:]):
                base = 0
                for start, count in parts:
                    place = pl.ds(pl.multiple_of(base + owner * count, 128), count)
                    out[:, place] = refs[slot][:, start : start + count].astype(jnp.float32)
                    base += LANES * count

    totals = [LANES * sum(count for _, count in parts) for parts in splits]
    return pl.pallas_call(
        kernel,
        grid_spec=pltpu.PrefetchScalarGridSpec(
            num_scalar_prefetch=1,
            grid=(rows // tile,),
            in_specs=[pl.BlockSpec((tile, columns), lambda i, _: (i, 0))] * LANES,
            out_specs=[pl.BlockSpec((tile, total), lambda i, _: (i, 0)) for total in totals],
        ),
        out_shape=[jax.ShapeDtypeStruct((rows, total), jnp.float32) for total in totals],
        cost_estimate=pl.CostEstimate(
            flops=0, transcendentals=0, bytes_accessed=6 * LANES * rows * columns
        ),
    )(lane.reshape(1), *slots)


def take_cols(weight, first, count):
    return lax.dynamic_slice_in_dim(weight, first, count, 1)


def on_device(
    tokens,
    cotangent,
    lengths,
    deal_order,
    attn_gain,
    mlp_gain,
    q_scale,
    k_scale,
    w_qkv,
    w_hgate,
    w_out,
    w_gate,
    w_up,
    w_down,
):
    f32, bf16 = jnp.float32, jnp.bfloat16
    rows = tokens.shape[1]
    width = tokens.shape[2]
    shards = lax.axis_size("fsdp")
    shard = lax.axis_index("fsdp")
    lane = lax.rem(lax.axis_index("rep"), LANES)
    group_list = QUERY_HEADS // KEY_VALUE_HEADS
    q_cols = group_list * HEAD_SIZE
    ff_cols = w_gate.shape[1] // LANES
    out_rows = w_out.shape[0]

    def padded(vector):
        return jnp.pad(vector, (0, out_rows - vector.shape[0]))[:, None]

    weights_one = jnp.concatenate(
        [
            take_cols(w_qkv, lane * q_cols, q_cols),
            take_cols(w_qkv, QUERY_HEADS * HEAD_SIZE + lane * HEAD_SIZE, HEAD_SIZE),
            take_cols(
                w_qkv, (QUERY_HEADS + KEY_VALUE_HEADS) * HEAD_SIZE + lane * HEAD_SIZE, HEAD_SIZE
            ),
            jnp.pad(
                jnp.concatenate(
                    [
                        take_cols(w_hgate, lane * group_list, group_list),
                        attn_gain[:, None],
                        mlp_gain[:, None],
                        padded(q_scale),
                        padded(k_scale),
                    ],
                    axis=1,
                ),
                ((0, 0), (0, 128 - group_list - 4)),
            ),
            take_cols(w_out, lane * q_cols, q_cols),
        ],
        axis=1,
    )
    weights_one = lax.all_gather(weights_one, "fsdp", axis=0, tiled=True)
    weights_two = lax.all_gather(
        jnp.concatenate(
            [take_cols(w_gate, lane * ff_cols, ff_cols), take_cols(w_up, lane * ff_cols, ff_cols)],
            axis=1,
        ),
        "fsdp",
        axis=0,
        tiled=True,
    )
    weights_three = lax.all_gather(
        take_cols(w_down, lane * ff_cols, ff_cols), "fsdp", axis=0, tiled=True
    )
    qkv_cols = q_cols + 2 * HEAD_SIZE
    w_in = weights_one[:, : qkv_cols + 128]
    w_attn = weights_one[:, qkv_cols + 128 :]
    extra = weights_one[:, qkv_cols : qkv_cols + group_list + 4].astype(f32)
    gain_one = extra[:, group_list]
    gain_two = extra[:, group_list + 1]
    scales = extra.reshape(shards, width // shards, group_list + 4)[:, : HEAD_SIZE // shards]
    query_gain = scales[:, :, group_list + 2].reshape(HEAD_SIZE)
    key_gain = scales[:, :, group_list + 3].reshape(HEAD_SIZE)

    seq_lengths = lengths[0]
    ends = jnp.cumsum(seq_lengths)
    starts = ends - seq_lengths
    own_index = shard * rows + jnp.arange(rows, dtype=jnp.int32)
    begun = own_index[:, None] >= starts[None, :]
    own_position = own_index - jnp.max(jnp.where(begun, starts[None, :], 0), axis=1)

    own_x = tokens[0]
    own_dy = cotangent[0]
    gathered = plane_gather(
        jnp.concatenate(
            [own_x, jnp.broadcast_to(own_position.astype(bf16)[:, None], (rows, 128))], axis=1
        )
    )
    stream_all = gathered[:, :width].astype(f32)
    position = gathered[:, width].astype(jnp.int32)
    cot_all = plane_gather(own_dy)
    total_rows = LANES * rows

    unit_all = normalize(stream_all)[0]
    normed_one = (unit_all * gain_one).astype(bf16)
    projected = matmul(normed_one, w_in)
    head_logit = projected[:, qkv_cols : qkv_cols + group_list]
    query_raw = projected[:, :q_cols].reshape(total_rows, group_list, HEAD_SIZE)
    key_raw = projected[:, q_cols : q_cols + HEAD_SIZE].reshape(total_rows, 1, HEAD_SIZE)
    values = projected[:, q_cols + HEAD_SIZE : qkv_cols].astype(bf16)
    query_unit, query_factor = normalize(query_raw)
    key_unit, key_factor = normalize(key_raw)
    cosine, sine_table = rope_tables(position)
    queries = (
        rotate(query_unit * query_gain, cosine, sine_table)
        .astype(bf16)
        .reshape(LANES, rows, group_list, HEAD_SIZE)
        .transpose(0, 2, 1, 3)
        .reshape(LANES, group_list * rows, HEAD_SIZE)
    )
    keys = rotate(key_unit * key_gain, cosine, sine_table).astype(bf16)
    key_value = jnp.concatenate([keys.reshape(total_rows, HEAD_SIZE), values], axis=1).reshape(
        LANES, rows, 2 * HEAD_SIZE
    )
    before = lax.ppermute(
        key_value[:, rows - HALO :], "fsdp", [(i, i + 1) for i in range(shards - 1)]
    )
    key_value = jnp.concatenate([before, key_value], axis=1)
    keys_wide = key_value[:, :, :HEAD_SIZE]
    values_wide = key_value[:, :, HEAD_SIZE:]
    local = jnp.arange(rows, dtype=jnp.int32)
    offset = jnp.arange(HALO + rows, dtype=jnp.int32) - HALO
    allowed = (offset[None, None, :] <= local[None, :, None]) & (
        offset[None, None, :] >= local[None, :, None] - position.reshape(LANES, rows)[:, :, None]
    )
    scores = jnp.einsum(
        "sqd,spd->sqp", queries, keys_wide, preferred_element_type=f32
    ) * HEAD_SIZE ** (-0.5)
    scores = jnp.where(jnp.concatenate([allowed] * group_list, axis=1), scores, -1e30)
    weights_exp = jnp.exp(scores - jnp.max(scores, axis=-1, keepdims=True))
    probs = weights_exp / jnp.sum(weights_exp, axis=-1, keepdims=True)
    probs_low = probs.astype(bf16)

    def by_row(value):
        return (
            value.reshape(LANES, group_list, rows, HEAD_SIZE)
            .transpose(0, 2, 1, 3)
            .reshape(total_rows, group_list, HEAD_SIZE)
        )

    def by_head(value):
        return (
            value.reshape(LANES, rows, group_list, HEAD_SIZE)
            .transpose(0, 2, 1, 3)
            .reshape(LANES, group_list * rows, HEAD_SIZE)
        )

    head_out = by_row(
        jnp.einsum("sqp,spd->sqd", probs_low, values_wide, preferred_element_type=f32)
    )
    head_gate = jax.nn.sigmoid(head_logit)
    gated = (head_out * head_gate[:, :, None]).astype(bf16).reshape(total_rows, q_cols)
    residual = own_x.astype(f32) + plane_scatter(contract_cols(gated, w_attn))
    unit_two, factor_two = normalize(residual)
    normed_two = plane_gather((unit_two * gain_two).astype(bf16))
    pre = matmul(normed_two, weights_two)
    gate_pre = pre[:, :ff_cols]
    up_pre = pre[:, ff_cols:]
    gate_sig = jax.nn.sigmoid(gate_pre)
    gate_act = gate_pre * gate_sig
    hidden = (gate_act * up_pre).astype(bf16)
    down_sum = OwnedSum(contract_rows(cot_all, hidden))
    down_sum.step()
    weights_three = down_sum.before(weights_three)
    down_sum.step()

    grad_hidden = matmul(cot_all, weights_three)
    grad_pre = jnp.concatenate(
        [
            (grad_hidden * up_pre * gate_sig * (1.0 + gate_pre * (1.0 - gate_sig))).astype(bf16),
            (grad_hidden * gate_act).astype(bf16),
        ],
        axis=1,
    )
    grad_pre = down_sum.before(grad_pre)
    down_sum = down_sum.total()
    pre_sum = OwnedSum(contract_rows(normed_two, grad_pre))
    grad_pre = pre_sum.step(grad_pre)
    contribution = plane_scatter(contract_cols(grad_pre, weights_two))
    grad_gain_two = jnp.sum(contribution * unit_two, axis=0)
    grad_resid = own_dy.astype(f32) + norm_back(contribution, unit_two, factor_two, gain_two)
    grad_branch = pre_sum.before(grad_resid.astype(bf16))
    for _ in range(shards - 3):
        pre_sum.step()
    grad_branch, down_sum = lax.optimization_barrier((plane_gather(grad_branch), down_sum))
    grad_gated = matmul(grad_branch, w_attn).reshape(total_rows, group_list, HEAD_SIZE)
    grad_heads = by_head((grad_gated * head_gate[:, :, None]).astype(bf16))
    grad_heads = pre_sum.before(grad_heads)
    grad_heads = pre_sum.step(grad_heads)
    down_all = plane_slots(down_sum)
    grad_logit = (jnp.sum(grad_gated * head_out, axis=-1) * head_gate * (1.0 - head_gate)).astype(
        bf16
    )
    grad_probs = jnp.einsum("sqd,spd->sqp", grad_heads, values_wide, preferred_element_type=f32)
    grad_values = jnp.einsum("sqp,sqd->spd", probs_low, grad_heads, preferred_element_type=f32)
    grad_scores = (
        probs * (grad_probs - jnp.sum(probs * grad_probs, axis=-1, keepdims=True))
    ).astype(bf16)
    grad_queries = (
        jnp.einsum("sqp,spd->sqd", grad_scores, keys_wide, preferred_element_type=f32)
        * HEAD_SIZE ** (-0.5)
    ).astype(bf16)
    grad_keys = jnp.einsum("sqp,sqd->spd", grad_scores, queries, preferred_element_type=f32)
    grad_key_value = jnp.concatenate([grad_keys, grad_values], axis=2)
    after = lax.ppermute(
        grad_key_value[:, :HALO].astype(bf16), "fsdp", [(i + 1, i) for i in range(shards - 1)]
    )
    grad_key_value = grad_key_value[:, HALO:] + jnp.pad(
        after.astype(f32), ((0, 0), (rows - HALO, 0), (0, 0))
    )
    grad_keys = (grad_key_value[:, :, :HEAD_SIZE] * HEAD_SIZE ** (-0.5)).astype(bf16)
    grad_values = grad_key_value[:, :, HEAD_SIZE:].reshape(total_rows, HEAD_SIZE)
    grad_query_rot = unrotate(by_row(grad_queries).astype(f32), cosine, sine_table)
    grad_key_rot = unrotate(
        grad_keys.astype(f32).reshape(total_rows, 1, HEAD_SIZE), cosine, sine_table
    )
    grad_query_gain = jnp.sum(grad_query_rot * query_unit, axis=(0, 1))
    grad_key_gain = jnp.sum(grad_key_rot * key_unit, axis=(0, 1))
    grad_query_raw = norm_back(grad_query_rot, query_unit, query_factor, query_gain)
    grad_key_raw = norm_back(grad_key_rot, key_unit, key_factor, key_gain)
    grad_projected = jnp.concatenate(
        [
            grad_query_raw.reshape(total_rows, q_cols),
            grad_key_raw.reshape(total_rows, HEAD_SIZE),
            grad_values,
            jnp.pad(grad_logit.astype(f32), ((0, 0), (0, 128 - group_list))),
        ],
        axis=1,
    ).astype(bf16)

    grad_projected = pre_sum.before(grad_projected)
    pre_all = plane_slots(pre_sum.total())
    grad_in = contract_rows(normed_one, grad_projected)
    partial_one = contract_cols(grad_projected, w_in)
    grad_gain_one = jnp.sum(partial_one * unit_all, axis=0)
    grad_out = contract_rows(grad_branch, gated)
    partial_one, grad_gain_one, grad_in, grad_out, hidden = lax.optimization_barrier(
        (partial_one, grad_gain_one, grad_in, grad_out, hidden)
    )
    grad_normed_one = plane_scatter(partial_one)
    final_rows = residual + plane_scatter(contract_cols(hidden, weights_three))
    final_rows = final_rows.astype(bf16)
    (w_down_grad,) = lay_out(lane, down_all, (((0, ff_cols),),))
    w_gate_grad, w_up_grad = lay_out(lane, pre_all, (((0, ff_cols),), ((ff_cols, ff_cols),)))
    unit_one, factor_one = normalize(own_x.astype(f32))
    grad_stream = grad_resid + norm_back(grad_normed_one, unit_one, factor_one, gain_one)

    scale_rows = width // shards

    def scale_column(vector):
        vector = vector.reshape(shards, HEAD_SIZE // shards)
        return jnp.pad(vector, ((0, 0), (0, scale_rows - HEAD_SIZE // shards))).reshape(width)

    extra_grads = jnp.stack(
        [grad_gain_one, grad_gain_two, scale_column(grad_query_gain), scale_column(grad_key_gain)]
    )
    places = jnp.arange(128)[None, :] == group_list + jnp.arange(4)[:, None]
    extra_grads = contract_rows(extra_grads.astype(bf16), places.astype(bf16))
    grad_in = grad_in + jnp.pad(extra_grads, ((0, 0), (qkv_cols, 0)))
    attn_sum = OwnedSum(
        jnp.concatenate([grad_in[:, :qkv_cols], grad_out, grad_in[:, qkv_cols:]], axis=1)
    )
    attn_all = plane_slots(attn_sum.total())
    w_qkv_grad, w_out_grad = lay_out(
        lane,
        attn_all,
        (
            ((0, q_cols), (q_cols, HEAD_SIZE), (q_cols + HEAD_SIZE, HEAD_SIZE)),
            ((qkv_cols, q_cols),),
        ),
    )
    small = jnp.stack([slot[:, qkv_cols + q_cols :] for slot in attn_all]).astype(f32)
    by_owner = [lax.dynamic_index_in_dim(small, lane ^ k, 0, False) for k in range(LANES)]
    sums = jnp.sum(small[:, :, group_list : group_list + 4], axis=0)
    return (
        final_rows[None],
        grad_stream.astype(bf16)[None],
        sums[:, 0],
        sums[:, 1],
        sums[: HEAD_SIZE // shards, 2],
        sums[: HEAD_SIZE // shards, 3],
        w_qkv_grad,
        jnp.concatenate([block[:, :group_list] for block in by_owner], axis=1),
        w_out_grad,
        w_gate_grad,
        w_up_grad,
        w_down_grad,
    )


def solution(mesh):
    return jax.shard_map(
        on_device,
        mesh=mesh,
        in_specs=(
            P("rep", "fsdp", None),
            P("rep", "fsdp", None),
            P("rep", None),
            P("rep", None),
            P("fsdp"),
            P("fsdp"),
            P("fsdp"),
            P("fsdp"),
            P("fsdp", None),
            P("fsdp", None),
            P("fsdp", None),
            P("fsdp", None),
            P("fsdp", None),
            P("fsdp", None),
        ),
        out_specs=(
            P("rep", "fsdp", None),
            P("rep", "fsdp", None),
            P("fsdp"),
            P("fsdp"),
            P("fsdp"),
            P("fsdp"),
            P("fsdp", None),
            P("fsdp", None),
            P("fsdp", None),
            P("fsdp", None),
            P("fsdp", None),
            P("fsdp", None),
        ),
        check_vma=False,
    )
```
